32 devices in a mesh: row: 8 (over z, core), col: 4 (over y, x).
Axes of the slice: x: 2, y: 2, z: 4, core: 2. Of those that a mesh axis runs over, the one named last changes fastest.
Arguments:
- coeffs: bfloat16 [256, 64, 128], P(('row', 'col')), may hold values from -6 to 6
- blocks: bfloat16 [16384, 64, 64], P(('row', 'col')), may hold values from -0.046875 to 0.046875
- blk_rows: int32 [16384], P(('row', 'col')), may hold values from 0 to 255, as said below
- blk_cols: int32 [16384], P(('row', 'col')), may hold values from 0 to 255, as said below
- blk_count: int32 [32], P(('row', 'col')), may hold values from 0 to 512, as said below
Outputs:
- product: float32 [256, 64, 128], P(('row', 'col'))
The draws below stay inside these ranges and needn't reach their ends.
Inputs may be any that keep to these rules, and one draw needn't show every extreme that they name: `blk_rows`: element e belongs to device e // 8 in row+col order. In the first blk_count slots of a device, I <= J, I belongs to a device of the same row index, and J to a device of the same column index whose row index exceeds that of I's device by 0 to 3; the difference 3 occurs in every draw. Later slots hold elements of the device's own row and column groups and are unused; pairs may repeat. `blk_cols`: see blk_rows. `blk_count`: counts differ widely between devices; some device uses all 512 slots in every draw.
All inputs are finite; a program needn't handle non-finite values.
Results may differ from the reference program's by a relative error of at most 0.0003.
Values may be sent and summed in bfloat16 or wider, within the bound.
No kernel may reach another device: no remote copies, remote signals or barrier semaphores. Data moves between devices by JAX's collectives and lax.ppermute only.
A program may use at most 128 MiB of HBM per device.

```python
import jax
import jax.numpy as jnp
from jax import lax

K = 64
NRHS = 128
ELEM_DEV = 8
BLK_DEV = 512
REACH = 3
ELEMS = 256
N_ROW = 8
N_COL = 4
DEVICES = 32


def layout(key):
    base = jax.random.fold_in(key, 4321)
    keys = jax.random.split(base, 6)
    device = jnp.arange(DEVICES, dtype=jnp.int32)[:, None]
    row_index = device // N_COL
    col_index = device % N_COL
    segment = ELEM_DEV * N_COL
    shape = (DEVICES, BLK_DEV)
    slots = jnp.arange(BLK_DEV, dtype=jnp.int32)[None, :]
    last_slot = (device == DEVICES - 1) & (slots == 0)
    row_elems = row_index * segment + jax.random.randint(keys[0], shape, 0, segment)
    row_elems = jnp.where(last_slot, ELEMS - 1, row_elems)
    offset = jax.random.randint(keys[1], shape, 0, REACH + 1)
    inside_block = jax.random.randint(keys[2], shape, 0, ELEM_DEV)
    inside_block = jnp.where(last_slot, ELEM_DEV - 1, inside_block)
    full_col = jax.random.randint(keys[3], (), 0, N_COL)
    offset = jnp.where((device == full_col) & (slots == 0), REACH, offset)
    first = (row_index * N_COL + col_index) * ELEM_DEV + inside_block
    offset = jnp.where((offset == 0) & (first < row_elems), REACH, offset)
    usable = row_index + offset <= N_ROW - 1
    col_elems = ((row_index + offset) * N_COL + col_index) * ELEM_DEV + inside_block
    col_elems = jnp.where(usable, col_elems, first)
    order = jnp.argsort(1 - usable.astype(jnp.int32), axis=1, stable=True)
    row_elems = jnp.take_along_axis(row_elems, order, axis=1)
    col_elems = jnp.take_along_axis(col_elems, order, axis=1)
    usable_total = jnp.sum(usable.astype(jnp.int32), axis=1)
    lowest = max(BLK_DEV // 16, 1)
    first_draw = jax.random.randint(keys[4], (DEVICES,), lowest, BLK_DEV + 1)
    second_draw = jax.random.randint(keys[5], (DEVICES,), lowest, BLK_DEV + 1)
    totals = jnp.minimum(first_draw, second_draw)
    totals = jnp.where(jnp.arange(DEVICES, dtype=jnp.int32) == full_col, BLK_DEV, totals)
    totals = jnp.minimum(totals, usable_total)
    return (row_elems.reshape(-1).astype(jnp.int32), col_elems.reshape(-1).astype(jnp.int32), totals.astype(jnp.int32))


def draw_blk_rows(key, part):
    return layout(key)[0]


def draw_blk_cols(key, part):
    return layout(key)[1]


def draw_blk_count(key, part):
    return layout(key)[2]


def block_scale(stream_key, dims, cuts, low, high):
    level = 1.0
    for position, parts in cuts:
        draws = jax.random.uniform(jax.random.fold_in(jax.random.fold_in(stream_key, 6), position), (parts,), jnp.float32, low / len(cuts), high / len(cuts))
        level = level * jnp.repeat(jnp.exp(draws), dims[position] // parts).reshape((-1,) + (1,) * (len(dims) - 1 - position))
    return level


def scatter_about(stream_key, extent, spread, limit, shards=(), kind=jnp.bfloat16):
    entries = spread * jax.random.normal(stream_key, extent, jnp.float32)
    if shards:
        entries = entries * block_scale(stream_key, extent, shards, -0.22, 0.18)
    return jnp.clip(entries, -limit, limit).astype(kind)


def setup_inputs(seed: int = 0) -> dict:
    splits = jax.random.split(jax.random.key(seed), 6)
    coeffs = scatter_about(splits[0], (ELEMS, K, NRHS), 1.0, 6.0, ((0, 32),))
    blocks = scatter_about(splits[1], (DEVICES * BLK_DEV, K, K), (K * BLK_DEV // 2) ** -0.5, 0.046875, ((0, 32),))
    blk_rows = draw_blk_rows(jax.random.fold_in(splits[5], 71), 0)
    blk_cols = draw_blk_cols(jax.random.fold_in(splits[5], 71), 0)
    blk_count = draw_blk_count(jax.random.fold_in(splits[5], 71), 0)
    return {"coeffs": coeffs, "blocks": blocks, "blk_rows": blk_rows, "blk_cols": blk_cols, "blk_count": blk_count}


def reference(coeffs, blocks, blk_rows, blk_cols, blk_count):
    high_precision = lax.Precision.HIGHEST
    segment = ELEM_DEV * N_COL
    all_blocks = blocks.reshape(DEVICES, BLK_DEV, K, K)
    all_rows = blk_rows.reshape(DEVICES, BLK_DEV)
    all_cols = blk_cols.reshape(DEVICES, BLK_DEV)
    slots = jnp.arange(BLK_DEV, dtype=jnp.int32)
    devices = jnp.arange(DEVICES, dtype=jnp.int32)
    seg_index = jnp.arange(segment, dtype=jnp.int32)

    def visit(total, inputs):
        upper_block_list, row_ids, column_numbers, used, device = inputs
        active = slots < used
        mirror = active & (row_ids != column_numbers)
        upper_block_list = upper_block_list.astype(jnp.float32)
        column_entries = coeffs[column_numbers].astype(jnp.float32)
        row_entries = coeffs[row_ids].astype(jnp.float32)
        row_contributions = jnp.einsum("gjc,gcx->gjx", upper_block_list, column_entries, precision=high_precision)
        column_contributions = jnp.einsum("ihv,ihe->ive", upper_block_list, row_entries, precision=high_precision)
        row_contributions = row_contributions * active.astype(jnp.float32)[:, None, None]
        column_contributions = column_contributions * mirror.astype(jnp.float32)[:, None, None]
        base = ((device // N_COL) * segment).astype(jnp.int32)
        row_local = jnp.clip(row_ids - base, 0, segment - 1).astype(jnp.int32)
        partial_value = jnp.zeros((segment, K, NRHS), jnp.float32).at[row_local].add(row_contributions)
        total = total.at[base + seg_index].add(partial_value)
        total = total.at[column_numbers].add(column_contributions)
        return total, None

    start = jnp.zeros((ELEMS, K, NRHS), jnp.float32)
    total, _ = lax.scan(visit, start, (all_blocks, all_rows, all_cols, blk_count, devices))
    return total
```

```python
import functools

import jax
import jax.numpy as jnp
from jax import lax
from jax.experimental import pallas as pl
from jax.experimental.pallas import tpu as pltpu
from jax.sharding import PartitionSpec as P

REACH = 3
TILE_SLOTS = 128
STEP_SLOTS = 64
TILE_MIB = 24
SUM_MIB = 24
CODE_ROWS = 16
VMEM = pltpu.VMEM
MIB = 1 << 20


def peers(axis):
    n = lax.axis_size(axis)
    if n & (n - 1) == 0:
        return range(1, n), lambda i, k: i ^ k
    return range(1, n), lambda i, k: (n + k - i) % n


def meet(x, axis, k):
    _, partner = peers(axis)
    return lax.ppermute(x, axis, [(i, partner(i, k)) for i in range(lax.axis_size(axis))])


def shift(x, axis, distance):
    devices = range(lax.axis_size(axis))
    return lax.ppermute(x, axis, [(i, i + distance) for i in devices if i + distance in devices])


def tiles_kernel(blocks_ref, tile_ref, flip_ref, narrow_ref, wide_ref, rows_ref, cols_ref, sems, *, width, slots):
    half = width // 2
    wpitch, spitch = width + 1, half + 1
    parts = blocks_ref.shape[1] // slots

    def fetch(part):
        return pltpu.make_async_copy(
            blocks_ref.at[:, pl.ds(part * slots, slots)], narrow_ref.at[part], sems.at[part]
        )

    for part in range(parts):
        fetch(part).start()

    for part in range(parts):
        fetch(part).wait()
        x_ref = narrow_ref.at[part]

        @pl.loop(0, width, unroll=8)
        def _(r):
            wide_ref[pl.ds(r * wpitch, width), :] = x_ref[
                pl.ds(pl.multiple_of(r * width, width), width), :
            ].astype(jnp.float32)

        @pl.loop(0, half, unroll=8)
        def _(q):
            pair = jnp.concatenate(
                [
                    x_ref[pl.ds(pl.multiple_of(q * width, width), width), :],
                    x_ref[pl.ds(pl.multiple_of((q + half) * width, width), width), :],
                ],
                axis=0,
            )
            rows_ref[pl.ds(q, slots, stride=spitch), :] = pair.astype(jnp.float32).T

        @pl.loop(0, half, unroll=8)
        def _(q):
            pair = jnp.concatenate(
                [
                    wide_ref[pl.ds(q, width, stride=wpitch), :],
                    wide_ref[pl.ds(q + half, width, stride=wpitch), :],
                ],
                axis=0,
            )
            cols_ref[pl.ds(q, slots, stride=spitch), :] = pair.T

        @pl.loop(0, slots, unroll=8)
        def _(s):
            at = pl.ds(pl.multiple_of((part * slots + s) * half, half), half)
            tile_ref[at, :] = rows_ref[pl.ds(s * spitch, half), :].astype(tile_ref.dtype)
            flip_ref[at, :] = cols_ref[pl.ds(s * spitch, half), :].astype(flip_ref.dtype)


def make_tiles(blocks):
    total, width, _ = blocks.shape
    slots, half = TILE_SLOTS, width // 2
    flat = blocks.transpose(1, 2, 0).reshape(width * width, total)
    flat = pltpu.with_memory_space_constraint(flat, pltpu.HBM)
    out = pltpu.VMEM((total * half, 2 * width), blocks.dtype)
    return pl.pallas_call(
        functools.partial(tiles_kernel, width=width, slots=slots),
        out_shape=[out, out],
        in_specs=[pl.BlockSpec(memory_space=pl.ANY)],
        out_specs=[pl.BlockSpec(memory_space=VMEM)] * 2,
        scratch_shapes=[
            VMEM((total // slots, width * width, slots), blocks.dtype),
            VMEM((width * (width + 1), slots), jnp.float32),
            VMEM((slots * (half + 1), 2 * width), jnp.float32),
            VMEM((slots * (half + 1), 2 * width), jnp.float32),
            pltpu.SemaphoreType.DMA((total // slots,)),
        ],
        compiler_params=pltpu.CompilerParams(vmem_limit_bytes=TILE_MIB * MIB),
        cost_estimate=pl.CostEstimate(flops=1 << 30, bytes_accessed=24 * MIB, transcendentals=0),
        name="tiles",
    )(flat)


def encode(total):
    elems, width, sides = total.shape
    top = jnp.maximum(jnp.max(jnp.abs(total), axis=1), 1e-30)
    power = jnp.floor(jnp.log2(top)) + 1.0
    codes = total * jnp.exp2(15.0 - power)[:, None, :]
    codes = jnp.clip(jnp.floor(codes + 0.5), -32767.0, 32767.0)
    power = jnp.concatenate([power, jnp.zeros((CODE_ROWS - elems, sides), jnp.float32)], axis=0)
    return codes, power


def products_kernel(count_ref, row_ref, col_ref, land_ref, tile_ref, flip_ref, *refs, reach, near):
    own_ref = refs[0]
    side_refs = refs[1 : 1 + near]
    far_refs = refs[1 + near : 1 + near + reach]
    outs = refs[1 + near + reach :]
    sum_ref = outs[0]
    side_outs = outs[1 : 1 + near]
    far_outs = outs[1 + near : 1 + near + reach]
    wrow_ref, wcol_ref, arow_ref, acol_ref = outs[1 + near + reach :]
    elems, width, sides = own_ref.shape
    half = width // 2
    me = lax.axis_index("col")
    steps, partner = peers("col")
    at_side = [partner(me, k) * elems for k in steps]
    for w_ref in (wrow_ref, wcol_ref):
        w_ref[:, 0:width, sides : 2 * sides] = jnp.zeros_like(w_ref[:, 0:width, sides : 2 * sides])
        w_ref[:, width : 2 * width, 0:sides] = jnp.zeros_like(w_ref[:, 0:width, 0:sides])

    def place(w_ref, at, ref):
        w_ref[pl.ds(at, elems), 0:width, 0:sides] = ref[...]
        w_ref[pl.ds(at, elems), width : 2 * width, sides : 2 * sides] = ref[...]

    place(wcol_ref, 0, own_ref)
    for d, ref in enumerate(far_refs):
        place(wcol_ref, (d + 1) * elems, ref)
    place(wrow_ref, me * elems, own_ref)
    for k, ref in enumerate(side_refs):
        place(wrow_ref, at_side[k], ref)
    arow_ref[...] = jnp.zeros_like(arow_ref)
    acol_ref[...] = jnp.zeros_like(acol_ref)

    @pl.loop(0, (count_ref[0] + STEP_SLOTS - 1) // STEP_SLOTS)
    def _(step):
        first = step * STEP_SLOTS
        for s in range(STEP_SLOTS):
            at = pl.ds(pl.multiple_of((first + s) * half, half), half)
            i, j, land = row_ref[first + s], col_ref[first + s], land_ref[first + s]
            d = jnp.dot(tile_ref[at, :], wcol_ref[j], preferred_element_type=jnp.float32)
            arow_ref[i, 0:half, :] += d[:, 0:sides]
            arow_ref[i, half:width, :] += d[:, sides : 2 * sides]
            d = jnp.dot(flip_ref[at, :], wrow_ref[i], preferred_element_type=jnp.float32)
            acol_ref[land, 0:half, :] += d[:, 0:sides]
            acol_ref[land, half:width, :] += d[:, sides : 2 * sides]

    sum_ref[...] = arow_ref[pl.ds(me * elems, elems)] + acol_ref[0:elems]
    pieces = [(o, acol_ref, (d + 1) * elems) for d, o in enumerate(far_outs)]
    pieces += [(o, arow_ref, at_side[k]) for k, o in enumerate(side_outs)]
    for o, a_ref, at in pieces:
        codes, power = encode(a_ref[pl.ds(at, elems)])
        o[0 : elems * width, :] = codes.reshape(elems * width, sides).astype(jnp.int32).astype(jnp.int16)
        o[elems * width : elems * width + CODE_ROWS, :] = power.astype(jnp.int32).astype(jnp.int16)


def products(count, row, col, land, tiles, flips, own, side, far):
    elems, width, sides = own.shape
    half = width // 2
    near, reach = len(side), len(far)
    group, window = (near + 1) * elems, (reach + 1) * elems
    code = jax.ShapeDtypeStruct((elems * width + CODE_ROWS, sides), jnp.int16)
    scalar, vector = pl.BlockSpec(memory_space=pltpu.SMEM), pl.BlockSpec(memory_space=VMEM)
    n_out = near + reach
    tiles, flips = (pltpu.with_memory_space_constraint(x, VMEM) for x in (tiles, flips))
    return pl.pallas_call(
        functools.partial(products_kernel, reach=reach, near=near),
        out_shape=[jax.ShapeDtypeStruct(own.shape, jnp.float32)] + [code] * n_out,
        in_specs=[scalar] * 4 + [vector] * (3 + n_out),
        out_specs=[vector] * (1 + n_out),
        scratch_shapes=[
            VMEM((group + 1, 2 * width, 2 * sides), own.dtype),
            VMEM((window + 1, 2 * width, 2 * sides), own.dtype),
            VMEM((group + 1, width, sides), jnp.float32),
            VMEM((window + 1, width, sides), jnp.float32),
        ],
        compiler_params=pltpu.CompilerParams(vmem_limit_bytes=SUM_MIB * MIB),
        cost_estimate=pl.CostEstimate(flops=1 << 32, bytes_accessed=24 * MIB, transcendentals=0),
        name="products",
    )(count, row, col, land, tiles, flips, own, *side, *far)


def finish_kernel(*refs):
    own_ref, codes, out_ref = refs[0], refs[1:-1], refs[-1]
    elems, width, sides = own_ref.shape
    total = own_ref[...]
    for ref in codes:
        power = ref[elems * width : elems * width + CODE_ROWS, :].astype(jnp.float32)[0:elems]
        value = ref[0 : elems * width, :].astype(jnp.float32).reshape(elems, width, sides)
        total = total + value * jnp.exp2(power - 15.0)[:, None, :]
    out_ref[...] = total


def finish(own, codes):
    vm = pl.BlockSpec(memory_space=VMEM)
    return pl.pallas_call(
        finish_kernel,
        out_shape=jax.ShapeDtypeStruct(own.shape, jnp.float32),
        in_specs=[vm] * (1 + len(codes)),
        out_specs=vm,
        compiler_params=pltpu.CompilerParams(vmem_limit_bytes=16 * MIB),
        name="finish",
    )(own, *codes)


def body(coeffs, blocks, blk_rows, blk_cols, blk_count):
    elems, width, sides = coeffs.shape
    total = blocks.shape[0]
    my_row = lax.axis_index("row")
    cols = lax.axis_size("col")
    segment, window = elems * cols, (REACH + 1) * elems
    steps, _ = peers("col")
    far = [shift(coeffs, "row", -d) for d in range(1, REACH + 1)]
    side = [meet(coeffs, "col", k) for k in steps]
    tiles, flips = make_tiles(blocks)
    active = jnp.arange(total, dtype=jnp.int32) < blk_count[0]
    row = jnp.clip(blk_rows - my_row * segment, 0, segment - 1)
    row = jnp.where(active, row, segment)
    col = (blk_cols // segment - my_row) * elems + blk_cols % elems
    col = jnp.clip(col, 0, window - 1)
    land = jnp.where(active & (blk_rows != blk_cols), col, window)
    own, *codes = products(blk_count, row, col, land, tiles, flips, coeffs, side, far)
    side_codes, far_codes = codes[: len(side)], codes[len(side) :]
    got = [shift(c, "row", d + 1) for d, c in enumerate(far_codes)]
    got += [meet(c, "col", k) for k, c in zip(steps, side_codes)]
    return finish(own, got)


def solution(mesh):
    placed = (
        P(("row", "col"), None, None),
        P(("row", "col"), None, None),
        P(("row", "col")),
        P(("row", "col")),
        P(("row", "col")),
    )
    return jax.shard_map(
        body, mesh=mesh, in_specs=placed, out_specs=P(("row", "col"), None, None), check_vma=False
    )
```

```python
import functools

import jax
import jax.numpy as jnp
from jax import lax
from jax.experimental import pallas as pl
from jax.experimental.pallas import tpu as pltpu
from jax.sharding import PartitionSpec as P

REACH = 3
TILE_SLOTS = 128
STEP_SLOTS = 64
TILE_MIB = 12
SUM_MIB = 8
UNROLL = 8
CODE_ROWS = 16
VMEM = pltpu.VMEM
MIB = 1 << 20


def peers(axis):
    n = lax.axis_size(axis)
    if n & (n - 1) == 0:
        return range(1, n), lambda i, k: i ^ k
    return range(1, n), lambda i, k: (n + k - i) % n


def meet(x, axis, k):
    _, partner = peers(axis)
    return lax.ppermute(x, axis, [(i, partner(i, k)) for i in range(lax.axis_size(axis))])


def shift(x, axis, distance):
    n = lax.axis_size(axis)
    return lax.ppermute(x, axis, [(i, (i + distance) % n) for i in range(n)])


def far_off(x):
    return pltpu.with_memory_space_constraint(x, pltpu.HBM)


def tiles_kernel(
    count_ref, own_hbm, rows_hbm, cols_hbm, blocks_ref, tile_ref, flip_ref, own_ref, row_ref, col_ref, land_ref,
    rows_ref, cols_ref, narrow_ref, wide_ref, sems,
    *, width, slots, elems
):
    half = width // 2
    wpitch, spitch = width + 1, half + 1
    parts = blocks_ref.shape[1] // slots

    def fetch(part):
        return pltpu.make_async_copy(
            blocks_ref.at[:, pl.ds(part * slots, slots)], narrow_ref.at[part], sems.at[part]
        )

    tables = [
        pltpu.make_async_copy(rows_hbm, rows_ref, sems.at[parts]),
        pltpu.make_async_copy(cols_hbm, cols_ref, sems.at[parts + 1]),
    ]
    own_copy = pltpu.make_async_copy(own_hbm, own_ref, sems.at[parts + 2])
    for copy in tables:
        copy.start()
    for part in range(parts):
        fetch(part).start()
    own_copy.start()
    for copy in tables:
        copy.wait()

    segment, window = elems * lax.axis_size("col"), (REACH + 1) * elems
    base = lax.axis_index("row") * segment
    shape = rows_ref.shape
    slot = lax.broadcasted_iota(jnp.int32, shape, 0) * shape[1] + lax.broadcasted_iota(jnp.int32, shape, 1)
    active = slot < count_ref[0]
    rows, cols = rows_ref[...], cols_ref[...]
    ahead = cols - base - lax.axis_index("col") * elems
    col = ahead
    for d in range(1, REACH + 1):
        col = col - jnp.where(ahead >= d * segment, segment - elems, 0)
    col = jnp.clip(col, 0, window - 1)
    row_ref[...] = jnp.where(active, jnp.clip(rows - base, 0, segment - 1), segment)
    col_ref[...] = col
    land_ref[...] = jnp.where(active & (rows != cols), col, window)

    for part in range(parts):
        fetch(part).wait()
        x_ref = narrow_ref.at[part]

        @pl.loop(0, half, unroll=UNROLL)
        def _(q):
            low = x_ref[pl.ds(pl.multiple_of(q * width, width), width), :].astype(jnp.float32)
            high = x_ref[pl.ds(pl.multiple_of((q + half) * width, width), width), :].astype(jnp.float32)
            wide_ref[pl.ds(q * wpitch, width), :] = low
            wide_ref[pl.ds((q + half) * wpitch, width), :] = high
            pair = jnp.concatenate([low, high], axis=0)
            tile_ref[pl.ds(part * slots * spitch + q, slots, stride=spitch), :] = pair.T

        @pl.loop(0, half, unroll=UNROLL)
        def _(q):
            low = wide_ref[pl.ds(q, width, stride=wpitch), :]
            high = wide_ref[pl.ds(q + half, width, stride=wpitch), :]
            pair = jnp.concatenate([low, high], axis=0).astype(x_ref.dtype)
            flip_ref[pl.ds(part * slots * spitch + q, slots, stride=spitch), :] = pair.T.astype(jnp.float32)

    own_copy.wait()


def make_tiles(count, rows, cols, blocks, own):
    total, width, _ = blocks.shape
    slots, half = TILE_SLOTS, width // 2
    flat = far_off(blocks.transpose(1, 2, 0).reshape(width * width, total))
    tiles = VMEM((total * (half + 1), 2 * width), jnp.float32)
    table = jax.ShapeDtypeStruct((total // 128, 128), jnp.int32)
    vector = pl.BlockSpec(memory_space=VMEM)
    tile, flip, own, *tables = pl.pallas_call(
        functools.partial(tiles_kernel, width=width, slots=slots, elems=own.shape[0]),
        out_shape=[tiles] * 2 + [VMEM(own.shape, own.dtype)] + [table] * 3,
        in_specs=[pl.BlockSpec(memory_space=pltpu.SMEM)] + [pl.BlockSpec(memory_space=pl.ANY)] * 4,
        out_specs=[vector] * 6,
        scratch_shapes=[
            VMEM(table.shape, jnp.int32),
            VMEM(table.shape, jnp.int32),
            VMEM((total // slots, width * width, slots), blocks.dtype),
            VMEM((width * (width + 1), slots), jnp.float32),
            pltpu.SemaphoreType.DMA((total // slots + 3,)),
        ],
        compiler_params=pltpu.CompilerParams(vmem_limit_bytes=TILE_MIB * MIB),
        cost_estimate=pl.CostEstimate(flops=1 << 30, bytes_accessed=24 * MIB, transcendentals=0),
        name="tiles",
    )(count, far_off(own), *(far_off(x.reshape(table.shape)) for x in (rows, cols)), flat)
    return tile, flip, own, [t.reshape(total) for t in tables]


def encode(total):
    elems, _, sides = total.shape
    top = jnp.maximum(jnp.max(jnp.abs(total), axis=1), 1e-30)
    power = jnp.floor(jnp.log2(top)) + 1.0
    codes = total * jnp.exp2(15.0 - power)[:, None, :]
    codes = jnp.clip(jnp.floor(codes + 0.5), -32767.0, 32767.0)
    power = jnp.concatenate([power, jnp.zeros((CODE_ROWS - elems, sides), jnp.float32)], axis=0)
    return codes, power


def put_codes(out_ref, total):
    elems, width, sides = total.shape
    codes, power = encode(total)
    out_ref[0 : elems * width, :] = codes.reshape(elems * width, sides).astype(jnp.int32).astype(jnp.int16)
    out_ref[elems * width : elems * width + CODE_ROWS, :] = power.astype(jnp.int32).astype(jnp.int16)


def products_kernel(count_ref, from_ref, to_ref, tile_ref, *refs, to_group, n_in, n_out):
    pieces, refs = refs[:n_in], refs[n_in:]
    more, refs = (refs[:1], refs[1:]) if to_group else ((), refs)
    sum_ref, outs, (x_ref, acc_ref) = refs[0], refs[1:n_out], refs[n_out:]
    elems, width, sides = pieces[0].shape
    half = width // 2
    me = lax.axis_index("col")
    steps, partner = peers("col")
    group = [me * elems] + [partner(me, k) * elems for k in steps]
    window = [d * elems for d in range(REACH + 1)]
    sources, places = (window, group) if to_group else (group, window)
    acc_ref[...] = jnp.zeros_like(acc_ref)
    for at, ref in zip(sources, pieces):
        x_ref[pl.ds(at, elems)] = ref[...]

    @pl.loop(0, (count_ref[0] + STEP_SLOTS - 1) // STEP_SLOTS)
    def _(step):
        first = step * STEP_SLOTS
        zero = jnp.zeros((width, sides), x_ref.dtype)
        for s in range(STEP_SLOTS):
            tile = tile_ref[pl.ds((first + s) * (half + 1), half), :].astype(x_ref.dtype)
            x, to = x_ref[from_ref[first + s]], to_ref[first + s]
            w = jnp.concatenate([jnp.concatenate([x, zero], axis=1), jnp.concatenate([zero, x], axis=1)], axis=0)
            d = jnp.dot(tile, w, preferred_element_type=jnp.float32)
            acc_ref[to, 0:half, :] += d[:, 0:sides]
            acc_ref[to, half:width, :] += d[:, sides : 2 * sides]

    total = acc_ref[pl.ds(places[0], elems)]
    for ref in more:
        total = total + ref[...]
    sum_ref[...] = total
    for at, ref in zip(places[1:], outs):
        put_codes(ref, acc_ref[pl.ds(at, elems)])


def products(count, source, target, tiles, pieces, n_out, more=()):
    elems, width, sides = pieces[0].shape
    n_in, to_group = len(pieces), bool(more)
    code = jax.ShapeDtypeStruct((elems * width + CODE_ROWS, sides), jnp.int16)
    scalar, vector = pl.BlockSpec(memory_space=pltpu.SMEM), pl.BlockSpec(memory_space=VMEM)
    return pl.pallas_call(
        functools.partial(products_kernel, to_group=to_group, n_in=n_in, n_out=n_out),
        out_shape=[jax.ShapeDtypeStruct((elems, width, sides), jnp.float32)] + [code] * (n_out - 1),
        in_specs=[scalar] * 3 + [vector] * (1 + n_in + len(more)),
        out_specs=[vector] * n_out,
        scratch_shapes=[
            VMEM((n_in * elems + 1, width, sides), pieces[0].dtype),
            VMEM((n_out * elems + 1, width, sides), jnp.float32),
        ],
        compiler_params=pltpu.CompilerParams(vmem_limit_bytes=SUM_MIB * MIB),
        cost_estimate=pl.CostEstimate(flops=1 << 31, bytes_accessed=12 * MIB, transcendentals=0),
        name="row_products" if to_group else "col_products",
    )(count, source, target, pltpu.with_memory_space_constraint(tiles, VMEM), *pieces, *more)


def finish_kernel(*refs):
    own_ref, codes, out_ref = refs[0], refs[1:-1], refs[-1]
    elems, width, sides = own_ref.shape
    total = own_ref[...]
    for ref in codes:
        power = ref[elems * width : elems * width + CODE_ROWS, :].astype(jnp.float32)[0:elems]
        value = ref[0 : elems * width, :].astype(jnp.float32).reshape(elems, width, sides)
        total = total + value * jnp.exp2(power - 15.0)[:, None, :]
    out_ref[...] = total


def finish(own, codes):
    vm = pl.BlockSpec(memory_space=VMEM)
    return pl.pallas_call(
        finish_kernel,
        out_shape=jax.ShapeDtypeStruct(own.shape, jnp.float32),
        in_specs=[vm] * (1 + len(codes)),
        out_specs=vm,
        compiler_params=pltpu.CompilerParams(vmem_limit_bytes=16 * MIB),
        name="finish",
    )(own, *codes)


def body(coeffs, blocks, blk_rows, blk_cols, blk_count):
    steps, _ = peers("col")
    reach = range(1, REACH + 1)
    side = [meet(coeffs, "col", k) for k in steps]
    far = [shift(coeffs, "row", -d) for d in reach]
    tiles, flips, mine, (row, col, land) = make_tiles(blk_count, blk_rows, blk_cols, blocks, coeffs)
    own, *codes = products(blk_count, row, land, flips, [mine] + side, 1 + len(far))
    got = []
    for d, c in zip(reach, codes):
        got.append(shift(c, "row", d))
    own, *codes = products(blk_count, col, row, tiles, [mine] + far, 1 + len(side), [own])
    got += [meet(c, "col", k) for k, c in zip(steps, codes)]
    return finish(own, got)


def solution(mesh):
    placed = (
        P(("row", "col"), None, None),
        P(("row", "col"), None, None),
        P(("row", "col")),
        P(("row", "col")),
        P(("row", "col")),
    )
    return jax.shard_map(
        body, mesh=mesh, in_specs=placed, out_specs=P(("row", "col"), None, None), check_vma=False
    )
```

```python
import functools

import jax
import jax.numpy as jnp
from jax import lax
from jax.experimental import pallas as pl
from jax.experimental.pallas import tpu as pltpu
from jax.sharding import PartitionSpec as P

REACH = 3
TILE_SLOTS = 128
STEP_SLOTS = 128
SHARE = 4
CHAINS = 2
LANES = 128
TILE_MIB = 12
SUM_MIB = 12
UNROLL = 8
CODE_ROWS = 16
VMEM = pltpu.VMEM
MIB = 1 << 20


def peers(axis):
    n = lax.axis_size(axis)
    if n & (n - 1) == 0:
        return range(1, n), lambda i, k: i ^ k
    return range(1, n), lambda i, k: (n + k - i) % n


def meet(x, axis, k):
    _, partner = peers(axis)
    return lax.ppermute(x, axis, [(i, partner(i, k)) for i in range(lax.axis_size(axis))])


def shift(x, axis, distance):
    n = lax.axis_size(axis)
    return lax.ppermute(x, axis, [(i, (i + distance) % n) for i in range(n)])


def far_off(x):
    return pltpu.with_memory_space_constraint(x, pltpu.HBM)


def places_for(total, keys):
    return -(-(total + keys * (SHARE - 1)) // LANES) * LANES


def order_slots(keys, active, dest, n_keys, nowhere, pitch, slot_ref, key_ref, dest_ref, steps_ref):
    blocks = keys.shape[0]
    places = slot_ref.shape[0] * LANES
    keys = jnp.where(active, keys, -1)
    lane = functools.partial(lax.broadcasted_iota, jnp.int32)
    which = lane((n_keys, LANES), 0)
    hits = [(jnp.broadcast_to(keys[b : b + 1], which.shape) == which).astype(jnp.float32) for b in range(blocks)]
    before = lane((LANES, 2 * LANES), 0) < lane((LANES, 2 * LANES), 1)
    before = before | (lane((LANES, 2 * LANES), 1) >= LANES)
    counts = jnp.dot(
        jnp.concatenate(hits, axis=0).astype(jnp.bfloat16),
        before.astype(jnp.float32).astype(jnp.bfloat16),
        preferred_element_type=jnp.float32,
    )
    seen, ranks = jnp.zeros((n_keys, LANES), jnp.float32), []
    for b in range(blocks):
        at = slice(b * n_keys, (b + 1) * n_keys)
        ranks.append(counts[at, 0:LANES] + seen)
        seen = seen + counts[at, LANES : 2 * LANES]
    chunks = jnp.floor((seen + (SHARE - 1)) * (1.0 / SHARE))
    lower = (lane((n_keys, n_keys), 1) < lane((n_keys, n_keys), 0)).astype(jnp.float32).astype(jnp.bfloat16)
    first = SHARE * jnp.dot(lower, chunks.astype(jnp.bfloat16), preferred_element_type=jnp.float32)
    place = [jnp.sum(h * (r + first + 1.0), axis=0, keepdims=True) - 1.0 for h, r in zip(hits, ranks)]
    turned = jnp.concatenate(place + [jnp.zeros((LANES - blocks, LANES), jnp.float32)], axis=0).T
    spread = lane((LANES, places), 1).astype(jnp.float32)
    found = jnp.zeros((8, places), jnp.float32)
    for b in range(blocks):
        chosen = (turned[:, b : b + 1] == spread).astype(jnp.float32).astype(jnp.bfloat16)
        row = lane((8, LANES), 0)
        value = jnp.where(row == 0, lane((8, LANES), 1), jnp.where(row == 1, b, 1))
        value = jnp.where(row == 2, jnp.broadcast_to(dest[b : b + 1], value.shape), value)
        value = jnp.where(row == 3, jnp.broadcast_to(keys[b : b + 1], value.shape), value)
        value = value.astype(jnp.float32).astype(jnp.bfloat16)
        found = found + jnp.dot(value, chosen, preferred_element_type=jnp.float32)
    found = found.astype(jnp.int32)
    slot = (found[0:1] + LANES * found[1:2]) * pitch
    to = jnp.where(found[4:5] > 0, found[2:3], nowhere)
    for i in range(places // LANES):
        at = slice(i * LANES, (i + 1) * LANES)
        slot_ref[i : i + 1, :] = slot[:, at]
        key_ref[i : i + 1, :] = found[3:4, at]
        dest_ref[i : i + 1, :] = to[:, at]
    used = jnp.sum(chunks, axis=0, keepdims=True) * SHARE
    steps_ref[...] = jnp.floor((used + (STEP_SLOTS - 1)) * (1.0 / STEP_SLOTS)).astype(jnp.int32)


def tiles_kernel(
    count_ref, own_hbm, rows_hbm, cols_hbm, blocks_ref, tile_ref, flip_ref, own_ref, *refs,
    width, slots, elems
):
    group_order, window_order, (rows_ref, cols_ref, narrow_ref, wide_ref, sems) = refs[:4], refs[4:8], refs[8:]
    half = width // 2
    wpitch, spitch = width + 1, half + 1
    parts = blocks_ref.shape[1] // slots

    def fetch(part):
        return pltpu.make_async_copy(
            blocks_ref.at[:, pl.ds(part * slots, slots)], narrow_ref.at[part], sems.at[part]
        )

    tables = [
        pltpu.make_async_copy(rows_hbm, rows_ref, sems.at[parts]),
        pltpu.make_async_copy(cols_hbm, cols_ref, sems.at[parts + 1]),
    ]
    own_copy = pltpu.make_async_copy(own_hbm, own_ref, sems.at[parts + 2])
    for copy in tables:
        copy.start()
    for part in range(parts):
        fetch(part).start()
    own_copy.start()
    for copy in tables:
        copy.wait()

    segment, window = elems * lax.axis_size("col"), (REACH + 1) * elems
    base = lax.axis_index("row") * segment
    shape = rows_ref.shape
    slot = lax.broadcasted_iota(jnp.int32, shape, 0) * shape[1] + lax.broadcasted_iota(jnp.int32, shape, 1)
    active = slot < count_ref[0]
    rows, cols = rows_ref[...], cols_ref[...]
    ahead = cols - base - lax.axis_index("col") * elems
    col = ahead
    for d in range(1, REACH + 1):
        col = col - jnp.where(ahead >= d * segment, segment - elems, 0)
    col = jnp.clip(col, 0, window - 1)
    row = jnp.clip(rows - base, 0, segment - 1)
    order_slots(row, active & (rows != cols), col, segment, window, spitch, *group_order)
    order_slots(col, active, row, window, segment, spitch, *window_order)

    for part in range(parts):
        fetch(part).wait()
        x_ref = narrow_ref.at[part]

        @pl.loop(0, half, unroll=UNROLL)
        def _(q):
            low = x_ref[pl.ds(pl.multiple_of(q * width, width), width), :].astype(jnp.float32)
            high = x_ref[pl.ds(pl.multiple_of((q + half) * width, width), width), :].astype(jnp.float32)
            wide_ref[pl.ds(q * wpitch, width), :] = low
            wide_ref[pl.ds((q + half) * wpitch, width), :] = high
            pair = jnp.concatenate([low, high], axis=0)
            tile_ref[pl.ds(part * slots * spitch + q, slots, stride=spitch), :] = pair.T

        @pl.loop(0, half, unroll=UNROLL)
        def _(q):
            low = wide_ref[pl.ds(q, width, stride=wpitch), :]
            high = wide_ref[pl.ds(q + half, width, stride=wpitch), :]
            pair = jnp.concatenate([low, high], axis=0).astype(x_ref.dtype)
            flip_ref[pl.ds(part * slots * spitch + q, slots, stride=spitch), :] = pair.T.astype(jnp.float32)

    own_copy.wait()


def make_tiles(count, rows, columns, blocks, own):
    total, width, _ = blocks.shape
    slots, half = TILE_SLOTS, width // 2
    flat = far_off(blocks.transpose(1, 2, 0).reshape(width * width, total))
    tiles = VMEM((total * (half + 1), 2 * width), jnp.float32)
    table = jax.ShapeDtypeStruct((total // LANES, LANES), jnp.int32)
    elems, cols = own.shape[0], lax.axis_size("col")
    orders = []
    for keys in (elems * cols, elems * (REACH + 1)):
        orders += [jax.ShapeDtypeStruct((places_for(total, keys) // LANES, LANES), jnp.int32)] * 3
        orders += [jax.ShapeDtypeStruct((1, LANES), jnp.int32)]
    vector = pl.BlockSpec(memory_space=VMEM)
    tile, flip, own, *orders = pl.pallas_call(
        functools.partial(tiles_kernel, width=width, slots=slots, elems=own.shape[0]),
        out_shape=[tiles] * 2 + [VMEM(own.shape, own.dtype)] + orders,
        in_specs=[pl.BlockSpec(memory_space=pltpu.SMEM)] + [pl.BlockSpec(memory_space=pl.ANY)] * 4,
        out_specs=[vector] * (3 + len(orders)),
        scratch_shapes=[
            VMEM(table.shape, jnp.int32),
            VMEM(table.shape, jnp.int32),
            VMEM((total // slots, width * width, slots), blocks.dtype),
            VMEM((width * (width + 1), slots), jnp.float32),
            pltpu.SemaphoreType.DMA((total // slots + 3,)),
        ],
        compiler_params=pltpu.CompilerParams(vmem_limit_bytes=TILE_MIB * MIB),
        cost_estimate=pl.CostEstimate(flops=1 << 30, bytes_accessed=24 * MIB, transcendentals=0),
        name="tiles",
    )(count, far_off(own), *(far_off(x.reshape(table.shape)) for x in (rows, columns)), flat)
    return tile, flip, own, orders[:4], orders[4:]


def encode(total):
    elems, _, sides = total.shape
    top = jnp.maximum(jnp.max(jnp.abs(total), axis=1), 1e-30)
    power = jnp.floor(jnp.log2(top)) + 1.0
    codes = total * jnp.exp2(15.0 - power)[:, None, :]
    codes = jnp.clip(jnp.floor(codes + 0.5), -32767.0, 32767.0)
    power = jnp.concatenate([power, jnp.zeros((CODE_ROWS - elems, sides), jnp.float32)], axis=0)
    return codes, power


def put_codes(out_ref, total):
    elems, width, sides = total.shape
    codes, power = encode(total)
    out_ref[0 : elems * width, :] = codes.reshape(elems * width, sides).astype(jnp.int32).astype(jnp.int16)
    out_ref[elems * width : elems * width + CODE_ROWS, :] = power.astype(jnp.int32).astype(jnp.int16)


def products_kernel(slot_ref, key_ref, to_ref, steps_ref, tile_ref, *refs, to_group, n_in, n_out):
    pieces, refs = refs[:n_in], refs[n_in:]
    more, refs = (refs[:1], refs[1:]) if to_group else ((), refs)
    sum_ref, outs, x_ref, accs = refs[0], refs[1:n_out], refs[n_out], refs[n_out + 1 :]
    elems, width, sides = pieces[0].shape
    half = width // 2
    me = lax.axis_index("col")
    steps, partner = peers("col")
    group = [me * elems] + [partner(me, k) * elems for k in steps]
    window = [d * elems for d in range(REACH + 1)]
    sources, places = (window, group) if to_group else (group, window)
    for acc_ref in accs:
        acc_ref[...] = jnp.zeros_like(acc_ref)
    for at, ref in zip(sources, pieces):
        x_ref[pl.ds(at, elems)] = ref[...]

    @pl.loop(0, steps_ref[0, 0])
    def _(step):
        row, lane = step // (LANES // STEP_SLOTS), step % (LANES // STEP_SLOTS) * STEP_SLOTS
        zero = jnp.zeros((width, sides), x_ref.dtype)
        for at in range(0, STEP_SLOTS, SHARE):
            x = x_ref[key_ref[row, lane + at]]
            w = jnp.concatenate([jnp.concatenate([x, zero], axis=1), jnp.concatenate([zero, x], axis=1)], axis=0)
            tiles = [tile_ref[pl.ds(slot_ref[row, lane + at + k], half), :] for k in range(SHARE)]
            d = jnp.dot(
                jnp.concatenate(tiles, axis=0).astype(x_ref.dtype), w, preferred_element_type=jnp.float32
            )
            for k in range(SHARE):
                to, one, acc_ref = to_ref[row, lane + at + k], slice(k * half, (k + 1) * half), accs[k % CHAINS]
                acc_ref[to, 0:half, :] += d[one, 0:sides]
                acc_ref[to, half:width, :] += d[one, sides : 2 * sides]

    def summed(at):
        return sum(acc_ref[pl.ds(at, elems)] for acc_ref in accs)

    total = summed(places[0])
    for ref in more:
        total = total + ref[...]
    sum_ref[...] = total
    for at, ref in zip(places[1:], outs):
        put_codes(ref, summed(at))


def products(order, tiles, pieces, n_out, more=()):
    elems, width, sides = pieces[0].shape
    n_in, to_group = len(pieces), bool(more)
    code = jax.ShapeDtypeStruct((elems * width + CODE_ROWS, sides), jnp.int16)
    scalar, vector = pl.BlockSpec(memory_space=pltpu.SMEM), pl.BlockSpec(memory_space=VMEM)
    return pl.pallas_call(
        functools.partial(products_kernel, to_group=to_group, n_in=n_in, n_out=n_out),
        out_shape=[jax.ShapeDtypeStruct((elems, width, sides), jnp.float32)] + [code] * (n_out - 1),
        in_specs=[scalar] * 4 + [vector] * (1 + n_in + len(more)),
        out_specs=[vector] * n_out,
        scratch_shapes=[
            VMEM((n_in * elems + 1, width, sides), pieces[0].dtype),
        ]
        + [VMEM((n_out * elems + 1, width, sides), jnp.float32)] * CHAINS,
        compiler_params=pltpu.CompilerParams(vmem_limit_bytes=SUM_MIB * MIB),
        cost_estimate=pl.CostEstimate(flops=1 << 31, bytes_accessed=12 * MIB, transcendentals=0),
        name="row_products" if to_group else "col_products",
    )(*order, pltpu.with_memory_space_constraint(tiles, VMEM), *pieces, *more)


def finish_kernel(*refs):
    own_ref, codes, out_ref = refs[0], refs[1:-1], refs[-1]
    elems, width, sides = own_ref.shape
    total = own_ref[...]
    for ref in codes:
        power = ref[elems * width : elems * width + CODE_ROWS, :].astype(jnp.float32)[0:elems]
        value = ref[0 : elems * width, :].astype(jnp.float32).reshape(elems, width, sides)
        total = total + value * jnp.exp2(power - 15.0)[:, None, :]
    out_ref[...] = total


def finish(own, codes):
    vm = pl.BlockSpec(memory_space=VMEM)
    return pl.pallas_call(
        finish_kernel,
        out_shape=jax.ShapeDtypeStruct(own.shape, jnp.float32),
        in_specs=[vm] * (1 + len(codes)),
        out_specs=vm,
        compiler_params=pltpu.CompilerParams(vmem_limit_bytes=16 * MIB),
        name="finish",
    )(own, *codes)


def body(coeffs, blocks, blk_rows, blk_cols, blk_count):
    steps, _ = peers("col")
    reach = range(1, REACH + 1)
    side = [meet(coeffs, "col", k) for k in steps]
    far = [shift(coeffs, "row", -d) for d in reach]
    tiles, flips, mine, by_group, by_window = make_tiles(blk_count, blk_rows, blk_cols, blocks, coeffs)
    own, *codes = products(by_group, flips, [mine] + side, 1 + len(far))
    got = []
    for d, c in zip(reach, codes):
        got.append(shift(c, "row", d))
    own, *codes = products(by_window, tiles, [mine] + far, 1 + len(side), [own])
    got += [meet(c, "col", k) for k, c in zip(steps, codes)]
    return finish(own, got)


def solution(mesh):
    placed = (
        P(("row", "col"), None, None),
        P(("row", "col"), None, None),
        P(("row", "col")),
        P(("row", "col")),
        P(("row", "col")),
    )
    return jax.shard_map(
        body, mesh=mesh, in_specs=placed, out_specs=P(("row", "col"), None, None), check_vma=False
    )
```
